32 devices in a mesh: bank: 8 (over z, y), grp: 4 (over x, core).
Axes of the slice: x: 2, y: 2, z: 4, core: 2. Of those that a mesh axis runs over, the one named last changes fastest.
Arguments:
- users: bfloat16 [4096, 256], P(('bank', 'grp')), may hold values from -32 to 32
- bank: bfloat16 [4096, 256], P('bank'), may hold values from -3 to 3
- positives: int32 [4096], P(('bank', 'grp')), may hold values from 0 to 4095
- cohorts: int32 [4096], P(('bank', 'grp')), may hold values from 0 to 15
Outputs:
- loss: float32 [], replicated
- user_grad: float32 [4096, 256], P(('bank', 'grp'))
- bank_grad: float32 [4096, 256], P(('bank', 'grp'))
The draws below stay inside these ranges and needn't reach their ends.
All inputs are finite; a program needn't handle non-finite values.
Results may differ from the reference program's by a relative error of at most 0.014.
Values may be sent and summed in bfloat16 or wider, within the bound.
A program may use at most 64 MiB of HBM per device.

```python
import math
import jax
import jax.numpy as jnp
import numpy as np
from jax import lax

E = 256
USER_DEV = 128
ITEM_DEV = 512
NCOH = 16
USERS = 4096
ITEMS = 4096
N_BANK = 8
N_GRP = 4


def bank_values(key):
    base = jax.random.normal(jax.random.fold_in(key, 11), (ITEMS, E), jnp.float32)
    values = 0.25 * jnp.clip(base, -6.0, 6.0)
    return jnp.clip(values, -3.0, 3.0)


def draw_bank(key, part):
    return bank_values(key).astype(jnp.bfloat16)


def draw_users(key, part):
    base = jax.random.normal(jax.random.fold_in(key, 21), (USERS, E), jnp.float32)
    values = 0.75 * jnp.clip(base, -6.0, 6.0)
    return jnp.clip(values, -32.0, 32.0).astype(jnp.bfloat16)


def plant(array, key, smallest, largest):
    spot = [jax.random.randint(jax.random.fold_in(key, axis), (), 0, length) for axis, length in enumerate(array.shape)]
    widest = array.shape.index(max(array.shape))
    next_to = spot[:widest] + [(spot[widest] + 1) % array.shape[widest]] + spot[widest + 1:]
    return array.at[tuple(spot)].set(smallest).at[tuple(next_to)].set(largest)


def cumulative_ranks(number_of, slope):
    loads = [(1 << 20) // math.isqrt(standing ** slope) + 1 for standing in range(1, number_of + 1)]
    scale = 1 + sum(loads) // (1 << 30)
    return np.cumsum(np.array([max(1, weight // scale) for weight in loads]))


def ranked(own_key, dims, number_of, slope):
    grid = cumulative_ranks(number_of, slope)
    ticket = jax.random.randint(jax.random.fold_in(own_key, 1), dims, 0, int(grid[number_of - 1]))
    standing = jnp.searchsorted(jnp.asarray(grid, jnp.int32), ticket, side="right")
    return jax.random.permutation(jax.random.fold_in(own_key, 2), number_of)[standing].astype(jnp.int32)


def setup_inputs(seed: int = 0) -> dict:
    splits = jax.random.split(jax.random.key(seed), 5)
    users = draw_users(jax.random.fold_in(splits[4], 71), 0)
    bank = draw_bank(jax.random.fold_in(splits[4], 71), 0)
    positives = plant(jax.random.randint(splits[2], (USERS,), 0, ITEMS), jax.random.fold_in(splits[2], 1), 0, ITEMS - 1).astype(jnp.int32)
    cohorts = plant(ranked(splits[3], (USERS,), NCOH, 2), jax.random.fold_in(splits[3], 3), 0, NCOH - 1).astype(jnp.int32)
    return dict(users=users, bank=bank, positives=positives, cohorts=cohorts)


def group_pass(users_g, pos_g, coh_g, bank, counts):
    rows = users_g.shape[0]
    block = 512 if rows % 512 == 0 else rows
    count = rows // block
    ub = users_g.reshape(count, block, E)
    pb = pos_g.reshape(count, block)
    cb = coh_g.reshape(count, block)
    cohort_ids = jnp.arange(NCOH, dtype=jnp.int32)
    item_ids = jnp.arange(ITEMS, dtype=jnp.int32)
    bank_blocks = bank.reshape(N_BANK, ITEM_DEV, E).astype(jnp.float32)
    scale = jnp.float32(USERS) / NCOH

    def step(carry, parts):
        upart, ppart, cpart = parts
        logits = jnp.dot(upart, bank.T, preferred_element_type=jnp.float32)
        top = jnp.max(logits, axis=1)
        lse = top + jnp.log(jnp.sum(jnp.exp(logits - top[:, None]), axis=1))
        hot = item_ids[None, :] == ppart[:, None]
        pos_logit = jnp.sum(jnp.where(hot, logits, jnp.float32(0.0)), axis=1)
        own = jnp.sum(jnp.where(cpart[:, None] == cohort_ids[None, :], counts[None, :], jnp.float32(0.0)), axis=1)
        weight = scale / own
        loss_part = jnp.sum(weight * (lse - pos_logit))
        prob = jnp.exp(logits - lse[:, None])
        dlogits = (weight[:, None] * (prob - hot.astype(jnp.float32))).astype(jnp.bfloat16)
        dblocks = dlogits.astype(jnp.float32).reshape(dlogits.shape[0], N_BANK, ITEM_DEV)
        terms = jnp.einsum("ubi,bie->bue", dblocks, bank_blocks, precision=lax.Precision.HIGHEST)
        rounded = lax.optimization_barrier(terms.astype(jnp.bfloat16))
        ugrad = jnp.sum(rounded.astype(jnp.float32), axis=0)
        bacc = carry[0] + jnp.dot(dlogits.astype(jnp.float32).T, upart.astype(jnp.float32), precision=lax.Precision.HIGHEST)
        return (bacc, carry[1] + loss_part), ugrad

    init = (jnp.zeros((ITEMS, E), jnp.float32), jnp.float32(0.0))
    (bacc, loss_sum), ugrads = lax.scan(step, init, (ub, pb, cb))
    return bacc, loss_sum, ugrads.reshape(rows, E)


def reference(users, bank, positives, cohorts):
    cohort_ids = jnp.arange(NCOH, dtype=jnp.int32)
    counts = jnp.sum((cohorts[:, None] == cohort_ids[None, :]).astype(jnp.float32), axis=0)
    ug = users.reshape(N_BANK, N_GRP, USER_DEV, E).transpose(1, 0, 2, 3).reshape(N_GRP, N_BANK * USER_DEV, E)
    pg = positives.reshape(N_BANK, N_GRP, USER_DEV).transpose(1, 0, 2).reshape(N_GRP, N_BANK * USER_DEV)
    cg = cohorts.reshape(N_BANK, N_GRP, USER_DEV).transpose(1, 0, 2).reshape(N_GRP, N_BANK * USER_DEV)

    def outer(carry, parts):
        bacc, loss_sum, ugrads = group_pass(parts[0], parts[1], parts[2], bank, counts)
        rounded = lax.optimization_barrier(bacc.astype(jnp.bfloat16)).astype(jnp.float32)
        return (carry[0] + rounded, carry[1] + loss_sum), ugrads

    init = (jnp.zeros((ITEMS, E), jnp.float32), jnp.float32(0.0))
    (bank_grad, loss_sum), ugrads = lax.scan(outer, init, (ug, pg, cg))
    user_grad = ugrads.reshape(N_GRP, N_BANK, USER_DEV, E).transpose(1, 0, 2, 3).reshape(USERS, E)
    loss = loss_sum / jnp.float32(USERS)
    return loss, user_grad, bank_grad
```

```python
import functools

import jax
import jax.numpy as jnp
from jax import lax
from jax.experimental import pallas as pl
from jax.experimental.pallas import tpu as pltpu
from jax.sharding import PartitionSpec as P

NCOH = 16
MESH = pl.DeviceIdType.MESH
F32 = jnp.float32
BF16 = jnp.bfloat16


def kernel(
    nz, ng, users_ref, bank_ref, pos_ref, coh_ref,
    loss_ref, ug_ref, bg_ref,
    allu, pbank, meta_own, meta, ex, dl,
    loc_max, loc_sum, loc_pos, stat, posl, cw, wt,
    hist, loss_buf, ug_send, ug_recv, bg_send, bg_recv,
    bank_sem, us, ur, ms, mr, ss, sr, ps, pr, gs, gr, hs, hr, ls, lr, bs, br,
):
    per_dev = users_ref.shape[0]
    items = bank_ref.shape[0]
    share = items // ng
    nq = 2 * ng
    me_b, me_g = lax.axis_index("bank"), lax.axis_index("grp")
    zc, par = me_b // 2, me_b % 2
    me_q = par * ng + me_g

    def col_id(z):
        return {"bank": 2 * z + par, "grp": me_g}

    def plane_id(q):
        return {"bank": 2 * zc + q // ng, "grp": q % ng}

    def col(k):
        return lax.rem(zc + k, nz)

    def plane(k):
        return lax.rem(me_q + k, nq)

    def rcopy(src, dst, send, recv, dev):
        return pltpu.make_async_remote_copy(
            src_ref=src, dst_ref=dst, send_sem=send, recv_sem=recv,
            device_id=dev, device_id_type=MESH,
        )

    def rows(z):
        return pl.ds(pl.multiple_of(z * per_dev, per_dev), per_dev)

    def users_cp(k, z, slot):
        return rcopy(users_ref, allu.at[rows(slot)], us.at[k], ur.at[slot], col_id(z))

    def meta_cp(k, z, slot):
        return rcopy(meta_own, meta.at[slot], ms.at[k], mr.at[slot], col_id(z))

    def stat_cp(k, z, slot):
        return rcopy(stat.at[zc], stat.at[slot], ss.at[k], sr.at[slot], col_id(z))

    def posl_cp(k, z, slot):
        return rcopy(posl.at[zc], posl.at[slot], ps.at[k], pr.at[slot], col_id(z))

    def ug_cp(k, z, slot):
        return rcopy(ug_send.at[k], ug_recv.at[slot], gs.at[k], gr.at[slot], col_id(z))

    def hist_cp(k, q, slot):
        return rcopy(hist.at[me_q], hist.at[slot], hs.at[k], hr.at[slot], plane_id(q))

    def loss_cp(k, q, slot):
        return rcopy(loss_buf.at[me_q], loss_buf.at[slot], ls.at[k], lr.at[slot], plane_id(q))

    def bg_cp(k, q, slot):
        return rcopy(bg_send.at[k], bg_recv.at[slot], bs.at[k], br.at[slot], plane_id(q))

    bank_cp = rcopy(
        bank_ref, pbank, bank_sem.at[0], bank_sem.at[1],
        {"bank": 2 * zc + 1 - par, "grp": me_g},
    )

    barrier = pltpu.get_barrier_semaphore()
    for k in range(1, nz):
        pl.semaphore_signal(barrier, inc=1, device_id=col_id(col(k)), device_id_type=MESH)
    for k in range(1, nq):
        pl.semaphore_signal(barrier, inc=1, device_id=plane_id(plane(k)), device_id_type=MESH)

    top_rows = lax.broadcasted_iota(jnp.int32, (8, per_dev), 0) == 0
    own_meta = jnp.where(top_rows, pos_ref[...], coh_ref[...])
    meta_own[...] = own_meta
    meta[zc] = own_meta
    allu[rows(zc), :] = users_ref[...]
    item_ids = lax.broadcasted_iota(jnp.int32, (items, per_dev), 0)
    banks = (bank_ref, pbank)
    base = (me_b * items, (2 * zc + 1 - par) * items)

    def hot_of(h, z):
        return item_ids == meta[z, 0:1, :] - base[h]

    def block(h, z):
        logits = lax.dot_general(
            banks[h][...], allu[rows(z), :], (((1,), (1,)), ((), ())),
            preferred_element_type=F32,
        )
        top = jnp.max(logits, axis=0, keepdims=True)
        e = jnp.exp(logits - top)
        ex[h, z] = e
        loc_max[h, pl.ds(z, 1), :] = top
        loc_sum[h, pl.ds(z, 1), :] = jnp.sum(e, axis=0, keepdims=True)
        loc_pos[h, pl.ds(z, 1), :] = jnp.sum(
            jnp.where(hot_of(h, z), logits, F32(0.0)), axis=0, keepdims=True
        )

    pl.semaphore_wait(barrier, nz - 1 + nq - 1)
    for k in range(1, nz):
        meta_cp(k, col(k), zc).start()
    for k in range(1, nz):
        users_cp(k, col(k), zc).start()
    bank_cp.start()
    block(0, zc)

    coh_ids = lax.broadcasted_iota(jnp.int32, (NCOH, per_dev), 0)
    for k in range(1, nz):
        z = col(nz - k)
        meta_cp(k, z, z).wait_recv()

    def count(z, acc):
        return acc + (coh_ids == meta[z, 1:2, :]).astype(F32)

    hist[me_q] = lax.fori_loop(0, nz, count, jnp.zeros((NCOH, per_dev), F32))
    for k in range(1, nq):
        hist_cp(k, plane(k), me_q).start()

    def first_half(k, carry):
        z = col(nz - k)
        users_cp(k, z, z).wait_recv()
        block(0, z)
        return carry

    lax.fori_loop(1, nz, first_half, 0)
    bank_cp.wait_recv()

    def second_half(z, carry):
        block(1, z)
        return carry

    lax.fori_loop(0, nz, second_half, 0)

    m0, m1 = loc_max[0], loc_max[1]
    m = jnp.maximum(m0, m1)
    s = loc_sum[0] * jnp.exp(m0 - m) + loc_sum[1] * jnp.exp(m1 - m)
    stat[zc, 0:nz, :] = m
    stat[zc, nz : 2 * nz, :] = s
    posl[zc] = jnp.zeros(posl.shape[1:], F32)
    posl[zc, 0:nz, :] = loc_pos[0] + loc_pos[1]
    for k in range(1, nz):
        stat_cp(k, col(k), zc).start()
    for k in range(1, nz):
        posl_cp(k, col(k), zc).start()

    for k in range(1, nq):
        q = plane(nq - k)
        hist_cp(k, q, q).wait_recv()
    total = hist[0]
    for q in range(1, nq):
        total = total + hist[q]
    counts = jnp.sum(total, axis=1, keepdims=True)
    scale = F32(per_dev * nz * nq) / NCOH

    def weigh(z, carry):
        own = jnp.sum(
            jnp.where(coh_ids == meta[z, 1:2, :], counts, F32(0.0)), axis=0, keepdims=True
        )
        wt[pl.ds(z, 1), :] = scale / own
        return carry

    lax.fori_loop(0, nz, weigh, 0)
    for k in range(1, nz):
        z = col(nz - k)
        stat_cp(k, z, z).wait_recv()
    top = stat[0, 0:nz, :]
    for z in range(1, nz):
        top = jnp.maximum(top, stat[z, 0:nz, :])
    tot = jnp.zeros_like(top)
    for z in range(nz):
        tot = tot + stat[z, nz : 2 * nz, :] * jnp.exp(stat[z, 0:nz, :] - top)
    lse = top + jnp.log(tot)
    cw[0] = wt[...] * jnp.exp(m0 - lse)
    cw[1] = wt[...] * jnp.exp(m1 - lse)

    def user_term(z):
        term = None
        for h in range(2):
            w = wt[pl.ds(z, 1), :]
            d = ex[h, z] * cw[h, pl.ds(z, 1), :] - jnp.where(hot_of(h, z), w, F32(0.0))
            d = d.astype(BF16)
            dl[h, :, rows(z)] = d
            part = lax.dot_general(
                d, banks[h][...], (((0,), (0,)), ((), ())), preferred_element_type=F32
            )
            term = part if term is None else term + part
        return term.astype(BF16)

    def peers_term(k, carry):
        z = col(k)
        ug_send[k] = user_term(z)
        ug_cp(k, z, zc).start()
        return carry

    lax.fori_loop(1, nz, peers_term, 0)
    ug_recv[zc] = user_term(zc)

    def bank_term(h, g):
        left = dl[h, pl.ds(pl.multiple_of(g * share, share), share), :]
        return jnp.dot(left, allu[...], preferred_element_type=F32).astype(BF16)

    for i in range(ng):
        g = lax.rem(me_g + i, ng)
        bg_send[i] = bank_term(1, g)
        bg_cp(i, (1 - par) * ng + g, me_q).start()
    for i in range(1, ng):
        g = lax.rem(me_g + i, ng)
        bg_send[ng + i] = bank_term(0, g)
        bg_cp(ng + i, par * ng + g, me_q).start()
    bg_recv[me_q] = bank_term(0, me_g)

    for k in range(1, nz):
        z = col(nz - k)
        posl_cp(k, z, z).wait_recv()
    pos = posl[0, 0:nz, :]
    for z in range(1, nz):
        pos = pos + posl[z, 0:nz, :]
    part = jnp.sum(wt[...] * (lse - pos), axis=0, keepdims=True)
    loss_buf[me_q] = jnp.broadcast_to(part, (8, per_dev))
    for k in range(1, nq):
        loss_cp(k, plane(k), me_q).start()

    for k in range(1, nz):
        z = col(nz - k)
        ug_cp(k, z, z).wait_recv()
    acc = ug_recv[0].astype(F32)
    for z in range(1, nz):
        acc = acc + ug_recv[z].astype(F32)
    ug_ref[...] = acc
    for k in range(1, nq):
        q = plane(nq - k)
        bg_cp(k, q, q).wait_recv()
    acc = bg_recv[0].astype(F32)
    for q in range(1, nq):
        acc = acc + bg_recv[q].astype(F32)
    bg_ref[...] = acc
    for k in range(1, nq):
        q = plane(nq - k)
        loss_cp(k, q, q).wait_recv()
    acc = loss_buf[0, 0:1, :]
    for q in range(1, nq):
        acc = acc + loss_buf[q, 0:1, :]
    loss_ref[...] = jnp.sum(acc, axis=1, keepdims=True) / F32(per_dev * nz * nq)

    bank_cp.wait_send()
    for k in range(1, nz):
        z = col(k)
        for cp in (users_cp, meta_cp, stat_cp, posl_cp, ug_cp):
            cp(k, z, zc).wait_send()
    for k in range(1, nq):
        q = plane(k)
        for cp in (hist_cp, loss_cp):
            cp(k, q, me_q).wait_send()
    for k in range(nq):
        if k != ng:
            bg_cp(k, plane(1), me_q).wait_send()


def solution(mesh):
    n_bank, ng = mesh.shape["bank"], mesh.shape["grp"]
    nz, nq = n_bank // 2, 2 * ng

    def per_device(users, bank, positives, cohorts):
        per_dev, width = users.shape
        items = bank.shape[0]
        share = items // ng
        padded = -(-nz // 8) * 8
        dma = pltpu.SemaphoreType.DMA
        vmem = pl.BlockSpec(memory_space=pltpu.VMEM)
        loss, ug, bg = pl.pallas_call(
            functools.partial(kernel, nz, ng),
            out_shape=(
                jax.ShapeDtypeStruct((1, 1), F32),
                jax.ShapeDtypeStruct((per_dev, width), F32),
                jax.ShapeDtypeStruct((share, width), F32),
            ),
            in_specs=[vmem] * 4,
            out_specs=(vmem, vmem, vmem),
            scratch_shapes=[
                pltpu.VMEM((nz * per_dev, width), BF16),
                pltpu.VMEM((items, width), BF16),
                pltpu.VMEM((8, per_dev), jnp.int32),
                pltpu.VMEM((nz, 8, per_dev), jnp.int32),
                pltpu.VMEM((2, nz, items, per_dev), F32),
                pltpu.VMEM((2, items, nz * per_dev), BF16),
                pltpu.VMEM((2, nz, per_dev), F32),
                pltpu.VMEM((2, nz, per_dev), F32),
                pltpu.VMEM((2, nz, per_dev), F32),
                pltpu.VMEM((nz, 2 * nz, per_dev), F32),
                pltpu.VMEM((nz, padded, per_dev), F32),
                pltpu.VMEM((2, nz, per_dev), F32),
                pltpu.VMEM((nz, per_dev), F32),
                pltpu.VMEM((nq, NCOH, per_dev), F32),
                pltpu.VMEM((nq, 8, per_dev), F32),
                pltpu.VMEM((nz, per_dev, width), BF16),
                pltpu.VMEM((nz, per_dev, width), BF16),
                pltpu.VMEM((nq, share, width), BF16),
                pltpu.VMEM((nq, share, width), BF16),
                dma((2,)),
                dma((nz,)), dma((nz,)), dma((nz,)), dma((nz,)), dma((nz,)),
                dma((nz,)), dma((nz,)), dma((nz,)), dma((nz,)), dma((nz,)),
                dma((nq,)), dma((nq,)), dma((nq,)), dma((nq,)), dma((nq,)), dma((nq,)),
            ],
            compiler_params=pltpu.CompilerParams(collective_id=0, has_side_effects=True),
        )(users, bank, positives.reshape(1, per_dev), cohorts.reshape(1, per_dev))
        return loss.reshape(()), ug, bg

    placed = (P(("bank", "grp"), None), P("bank", None), P(("bank", "grp")), P(("bank", "grp")))
    return jax.shard_map(
        per_device,
        mesh=mesh,
        in_specs=placed,
        out_specs=(P(), P(("bank", "grp"), None), P(("bank", "grp"), None)),
        check_vma=False,
    )
```

```python
import functools

import jax
import jax.numpy as jnp
from jax import lax
from jax.experimental import pallas as pl
from jax.experimental.pallas import tpu as pltpu
from jax.sharding import PartitionSpec as P

NCOH = 16
MESH = pl.DeviceIdType.MESH
F32 = jnp.float32
BF16 = jnp.bfloat16


def kernel(
    nz, ng, users_hbm, bank_hbm, pos_hbm, coh_hbm,
    loss_buf, ug_recv, bg_recv,
    allu, bank_ref, pbank, pos_ref, coh_ref, local, meta_own, meta, ex, dl,
    loc_max, loc_sum, loc_pos, stat, posl, cw, wt,
    hist, ug_send, bg_send,
    bank_sem, us, ur, ms, mr, ss, sr, ps, pr, gs, gr, hs, hr, ls, lr, bs, br,
):
    per_dev = users_hbm.shape[0]
    items = bank_hbm.shape[0]
    share = items // ng
    nq = 2 * ng
    me_b, me_g = lax.axis_index("bank"), lax.axis_index("grp")
    zc, par = me_b // 2, me_b % 2
    me_q = par * ng + me_g

    def col_id(z):
        return {"bank": 2 * z + par, "grp": me_g}

    def plane_id(q):
        return {"bank": 2 * zc + q // ng, "grp": q % ng}

    def col(k):
        down, up = nz - k, k - 1
        down = down - (zc - down + nz) // nz
        up = up + (up - zc + nz) // nz
        upper = (2 * zc) // nz
        return (1 - upper) * down + upper * up

    def plane(k):
        return lax.rem(me_q + k, nq)

    def rcopy(src, dst, send, recv, dev):
        return pltpu.make_async_remote_copy(
            src_ref=src, dst_ref=dst, send_sem=send, recv_sem=recv,
            device_id=dev, device_id_type=MESH,
        )

    def rows(z):
        return pl.ds(pl.multiple_of(z * per_dev, per_dev), per_dev)

    def users_cp(k, z, slot):
        return rcopy(allu.at[rows(zc)], allu.at[rows(slot)], us.at[k], ur.at[slot], col_id(z))

    def meta_cp(k, z, slot):
        return rcopy(meta_own, meta.at[slot], ms.at[k], mr.at[slot], col_id(z))

    def stat_cp(k, z, slot):
        return rcopy(stat.at[zc], stat.at[slot], ss.at[k], sr.at[slot], col_id(z))

    def posl_cp(k, z, slot):
        return rcopy(posl.at[zc], posl.at[slot], ps.at[k], pr.at[slot], col_id(z))

    def ug_cp(k, z, slot):
        return rcopy(ug_send.at[k], ug_recv.at[slot], gs.at[k], gr.at[slot], col_id(z))

    def hist_cp(k, q, slot):
        return rcopy(hist.at[me_q], hist.at[slot], hs.at[k], hr.at[slot], plane_id(q))

    def loss_cp(k, q, slot):
        return rcopy(loss_buf.at[me_q], loss_buf.at[slot], ls.at[k], lr.at[slot], plane_id(q))

    def bg_cp(k, q, slot):
        return rcopy(bg_send.at[k], bg_recv.at[slot], bs.at[k], br.at[slot], plane_id(q))

    bank_cp = rcopy(
        bank_ref, pbank, bank_sem.at[0], bank_sem.at[1],
        {"bank": 2 * zc + 1 - par, "grp": me_g},
    )

    barrier = pltpu.get_barrier_semaphore()
    for k in range(1, nz):
        pl.semaphore_signal(barrier, inc=1, device_id=col_id(col(k)), device_id_type=MESH)
    for k in range(1, nq):
        pl.semaphore_signal(barrier, inc=1, device_id=plane_id(plane(k)), device_id_type=MESH)

    loads = [
        pltpu.make_async_copy(src, dst, local.at[i])
        for i, (src, dst) in enumerate((
            (pos_hbm, pos_ref), (coh_hbm, coh_ref),
            (users_hbm, allu.at[rows(zc)]), (bank_hbm, bank_ref),
        ))
    ]
    for load in loads:
        load.start()
    for load in loads[:2]:
        load.wait()
    top_rows = lax.broadcasted_iota(jnp.int32, (8, per_dev), 0) == 0
    own_meta = jnp.where(top_rows, pos_ref[...], coh_ref[...])
    meta_own[...] = own_meta
    meta[zc] = own_meta
    item_ids = lax.broadcasted_iota(jnp.int32, (items, per_dev), 0)
    banks = (bank_ref, pbank)
    base = (me_b * items, (2 * zc + 1 - par) * items)

    def hot_of(h, z):
        return item_ids == meta[z, 0:1, :] - base[h]

    def block(h, z):
        logits = lax.dot_general(
            banks[h][...], allu[rows(z), :], (((1,), (1,)), ((), ())),
            preferred_element_type=F32,
        )
        top = jnp.max(logits, axis=0, keepdims=True)
        e = jnp.exp(logits - top)
        ex[h, z] = e
        loc_max[h, pl.ds(z, 1), :] = top
        loc_sum[h, pl.ds(z, 1), :] = jnp.sum(e, axis=0, keepdims=True)
        loc_pos[h, pl.ds(z, 1), :] = jnp.sum(
            jnp.where(hot_of(h, z), logits, F32(0.0)), axis=0, keepdims=True
        )

    for load in loads[2:]:
        load.wait()
    pl.semaphore_wait(barrier, nz - 1 + nq - 1)
    for k in range(1, nz):
        meta_cp(k, col(k), zc).start()
    for k in range(1, nz):
        users_cp(k, col(k), zc).start()
    bank_cp.start()
    block(0, zc)

    coh_ids = lax.broadcasted_iota(jnp.int32, (NCOH, per_dev), 0)
    for k in range(1, nz):
        z = col(nz - k)
        meta_cp(k, z, z).wait_recv()

    def count(z, acc):
        return acc + (coh_ids == meta[z, 1:2, :]).astype(F32)

    hist[me_q] = lax.fori_loop(0, nz, count, jnp.zeros((NCOH, per_dev), F32))
    for k in range(1, nq):
        hist_cp(k, plane(k), me_q).start()

    bank_cp.wait_recv()
    block(1, zc)

    def arriving(k, carry):
        z = col(nz - k)
        users_cp(k, z, z).wait_recv()
        block(0, z)
        block(1, z)
        return carry

    lax.fori_loop(1, nz, arriving, 0)

    m0, m1 = loc_max[0], loc_max[1]
    m = jnp.maximum(m0, m1)
    s = loc_sum[0] * jnp.exp(m0 - m) + loc_sum[1] * jnp.exp(m1 - m)
    stat[zc, 0:nz, :] = m
    stat[zc, nz : 2 * nz, :] = s
    posl[zc] = jnp.zeros(posl.shape[1:], F32)
    posl[zc, 0:nz, :] = loc_pos[0] + loc_pos[1]
    for k in range(1, nz):
        stat_cp(k, col(k), zc).start()
    for k in range(1, nz):
        posl_cp(k, col(k), zc).start()

    for k in range(1, nq):
        q = plane(nq - k)
        hist_cp(k, q, q).wait_recv()
    total = hist[0]
    for q in range(1, nq):
        total = total + hist[q]
    counts = jnp.sum(total, axis=1, keepdims=True)
    scale = F32(per_dev * nz * nq) / NCOH

    def weigh(z, carry):
        own = jnp.sum(
            jnp.where(coh_ids == meta[z, 1:2, :], counts, F32(0.0)), axis=0, keepdims=True
        )
        wt[pl.ds(z, 1), :] = scale / own
        return carry

    lax.fori_loop(0, nz, weigh, 0)
    for k in range(1, nz):
        z = col(nz - k)
        stat_cp(k, z, z).wait_recv()
    top = stat[0, 0:nz, :]
    for z in range(1, nz):
        top = jnp.maximum(top, stat[z, 0:nz, :])
    tot = jnp.zeros_like(top)
    for z in range(nz):
        tot = tot + stat[z, nz : 2 * nz, :] * jnp.exp(stat[z, 0:nz, :] - top)
    lse = top + jnp.log(tot)
    cw[0] = wt[...] * jnp.exp(m0 - lse)
    cw[1] = wt[...] * jnp.exp(m1 - lse)

    def dlogits(h, z):
        w = wt[pl.ds(z, 1), :]
        d = ex[h, z] * cw[h, pl.ds(z, 1), :] - jnp.where(hot_of(h, z), w, F32(0.0))
        dl[h, :, rows(z)] = d.astype(BF16)

    def user_term(z):
        term = None
        for h in range(2):
            part = lax.dot_general(
                dl[h, :, rows(z)], banks[h][...], (((0,), (0,)), ((), ())),
                preferred_element_type=F32,
            )
            term = part if term is None else term + part
        return term.astype(BF16)

    def peers_term(k, carry):
        z = col(k)
        dlogits(0, z)
        dlogits(1, z)
        ug_send[k] = user_term(z)
        ug_cp(k, z, zc).start()
        return carry

    lax.fori_loop(1, nz, peers_term, 0)
    dlogits(0, zc)
    dlogits(1, zc)

    def bank_term(h, g):
        left = dl[h, pl.ds(pl.multiple_of(g * share, share), share), :]
        return jnp.dot(left, allu[...], preferred_element_type=F32).astype(BF16)

    for i in range(ng):
        g = lax.rem(me_g + i, ng)
        bg_send[i] = bank_term(1, g)
        bg_cp(i, (1 - par) * ng + g, me_q).start()
    for i in range(1, ng):
        g = lax.rem(me_g + i, ng)
        bg_send[ng + i] = bank_term(0, g)
        bg_cp(ng + i, par * ng + g, me_q).start()
    bg_recv[me_q] = bank_term(0, me_g)
    ug_recv[zc] = user_term(zc)

    for k in range(1, nz):
        z = col(nz - k)
        posl_cp(k, z, z).wait_recv()
    pos = posl[0, 0:nz, :]
    for z in range(1, nz):
        pos = pos + posl[z, 0:nz, :]
    part = jnp.sum(wt[...] * (lse - pos), axis=0, keepdims=True)
    loss_buf[me_q] = jnp.broadcast_to(part, (8, per_dev))
    for k in range(1, nq):
        loss_cp(k, plane(k), me_q).start()

    for k in range(1, nz):
        z = col(nz - k)
        ug_cp(k, z, z).wait_recv()
    for k in range(1, nq):
        q = plane(nq - k)
        bg_cp(k, q, q).wait_recv()
    for k in range(1, nq):
        q = plane(nq - k)
        loss_cp(k, q, q).wait_recv()

    bank_cp.wait_send()
    for k in range(1, nz):
        z = col(k)
        for cp in (users_cp, meta_cp, stat_cp, posl_cp, ug_cp):
            cp(k, z, zc).wait_send()
    for k in range(1, nq):
        q = plane(k)
        for cp in (hist_cp, loss_cp):
            cp(k, q, me_q).wait_send()
    for k in range(nq):
        if k != ng:
            bg_cp(k, plane(1), me_q).wait_send()


def finish(users, loss_buf, ug_recv, bg_recv, loss_ref, ug_hbm, bg_hbm, ug, bg, sem):
    copies = []
    for i, (terms, total, out) in enumerate(((ug_recv, ug, ug_hbm), (bg_recv, bg, bg_hbm))):
        acc = terms[0].astype(F32)
        for t in range(1, terms.shape[0]):
            acc = acc + terms[t].astype(F32)
        total[...] = acc
        copies.append(pltpu.make_async_copy(total, out, sem.at[i]))
        copies[-1].start()
    acc = loss_buf[0, 0:1, :]
    for q in range(1, loss_buf.shape[0]):
        acc = acc + loss_buf[q, 0:1, :]
    loss_ref[...] = jnp.sum(acc, axis=1, keepdims=True) / F32(users)
    for copy in copies:
        copy.wait()


def solution(mesh):
    n_bank, ng = mesh.shape["bank"], mesh.shape["grp"]
    nz, nq = n_bank // 2, 2 * ng

    def per_device(users, bank, positives, cohorts):
        per_dev, width = users.shape
        items = bank.shape[0]
        share = items // ng
        padded = -(-nz // 8) * 8
        dma = pltpu.SemaphoreType.DMA
        vmem = pl.BlockSpec(memory_space=pltpu.VMEM)
        anywhere = pl.BlockSpec(memory_space=pl.ANY)
        received = pl.pallas_call(
            functools.partial(kernel, nz, ng),
            out_shape=(
                pltpu.VMEM((nq, 8, per_dev), F32),
                pltpu.VMEM((nz, per_dev, width), BF16),
                pltpu.VMEM((nq, share, width), BF16),
            ),
            in_specs=[anywhere] * 4,
            out_specs=(vmem, vmem, vmem),
            scratch_shapes=[
                pltpu.VMEM((nz * per_dev, width), BF16),
                pltpu.VMEM((items, width), BF16),
                pltpu.VMEM((items, width), BF16),
                pltpu.VMEM((1, per_dev), jnp.int32),
                pltpu.VMEM((1, per_dev), jnp.int32),
                dma((4,)),
                pltpu.VMEM((8, per_dev), jnp.int32),
                pltpu.VMEM((nz, 8, per_dev), jnp.int32),
                pltpu.VMEM((2, nz, items, per_dev), F32),
                pltpu.VMEM((2, items, nz * per_dev), BF16),
                pltpu.VMEM((2, nz, per_dev), F32),
                pltpu.VMEM((2, nz, per_dev), F32),
                pltpu.VMEM((2, nz, per_dev), F32),
                pltpu.VMEM((nz, 2 * nz, per_dev), F32),
                pltpu.VMEM((nz, padded, per_dev), F32),
                pltpu.VMEM((2, nz, per_dev), F32),
                pltpu.VMEM((nz, per_dev), F32),
                pltpu.VMEM((nq, NCOH, per_dev), F32),
                pltpu.VMEM((nz, per_dev, width), BF16),
                pltpu.VMEM((nq, share, width), BF16),
                dma((2,)),
                dma((nz,)), dma((nz,)), dma((nz,)), dma((nz,)), dma((nz,)),
                dma((nz,)), dma((nz,)), dma((nz,)), dma((nz,)), dma((nz,)),
                dma((nq,)), dma((nq,)), dma((nq,)), dma((nq,)), dma((nq,)), dma((nq,)),
            ],
            compiler_params=pltpu.CompilerParams(collective_id=0, has_side_effects=True),
        )(users, bank, positives.reshape(1, per_dev), cohorts.reshape(1, per_dev))
        loss, ug, bg = pl.pallas_call(
            functools.partial(finish, per_dev * nz * nq),
            out_shape=(
                jax.ShapeDtypeStruct((1, 1), F32),
                jax.ShapeDtypeStruct((per_dev, width), F32),
                jax.ShapeDtypeStruct((share, width), F32),
            ),
            in_specs=[vmem] * 3,
            out_specs=(vmem, anywhere, anywhere),
            scratch_shapes=[
                pltpu.VMEM((per_dev, width), F32),
                pltpu.VMEM((share, width), F32),
                dma((2,)),
            ],
        )(*(pltpu.with_memory_space_constraint(x, pltpu.VMEM) for x in received))
        return loss.reshape(()), ug, bg

    placed = (P(("bank", "grp"), None), P("bank", None), P(("bank", "grp")), P(("bank", "grp")))
    return jax.shard_map(
        per_device,
        mesh=mesh,
        in_specs=placed,
        out_specs=(P(), P(("bank", "grp"), None), P(("bank", "grp"), None)),
        check_vma=False,
    )
```

```python
import functools

import jax
import jax.numpy as jnp
from jax import lax
from jax.experimental import pallas as pl
from jax.experimental.pallas import tpu as pltpu
from jax.sharding import PartitionSpec as P

NCOH = 16
MESH = pl.DeviceIdType.MESH
F32 = jnp.float32
BF16 = jnp.bfloat16


def kernel(
    nz, ng, users_hbm, bank_hbm, pos_hbm, coh_hbm,
    loss_buf, ug_recv, bg_recv,
    allu, bank_ref, pbank, pos_ref, coh_ref, local, meta_own, meta, ex, dl,
    loc_max, loc_sum, loc_pos, stat, posl, cw, wt,
    hist, et, ht, ug_send, bg_send, pre_send, pre_recv,
    bank_sem, us, ur, ms, mr, ss, sr, ps, pr, gs, gr, hs, hr, ls, lr, bs, br, xs, xr,
):
    per_dev = users_hbm.shape[0]
    items = bank_hbm.shape[0]
    share = items // ng
    nq = 2 * ng
    me_b, me_g = lax.axis_index("bank"), lax.axis_index("grp")
    zc, par = me_b // 2, me_b % 2
    me_q = par * ng + me_g
    npair, half = ng // 2, items // 2
    pair, side = me_g // 2, me_g % 2
    nr = 2 * npair
    me_r = par * npair + pair
    sibling = {"bank": me_b, "grp": 2 * pair + 1 - side}

    def col_id(z):
        return {"bank": 2 * z + par, "grp": me_g}

    def plane_id(q):
        return {"bank": 2 * zc + q // ng, "grp": q % ng}

    def col(k):
        down, up = nz - k, k - 1
        down = down - (zc - down + nz) // nz
        up = up + (up - zc + nz) // nz
        upper = (2 * zc) // nz
        return (1 - upper) * down + upper * up

    def plane(k):
        return lax.rem(me_q + k, nq)

    def rcopy(src, dst, send, recv, dev):
        return pltpu.make_async_remote_copy(
            src_ref=src, dst_ref=dst, send_sem=send, recv_sem=recv,
            device_id=dev, device_id_type=MESH,
        )

    def rows(z):
        return pl.ds(pl.multiple_of(z * per_dev, per_dev), per_dev)

    def users_cp(k, z, slot):
        return rcopy(allu.at[rows(zc)], allu.at[rows(slot)], us.at[k], ur.at[slot], col_id(z))

    def meta_cp(k, z, slot):
        return rcopy(meta_own, meta.at[slot], ms.at[k], mr.at[slot], col_id(z))

    def stat_cp(k, z, slot):
        return rcopy(stat.at[zc], stat.at[slot], ss.at[k], sr.at[slot], col_id(z))

    def posl_cp(k, z, slot):
        return rcopy(posl.at[zc], posl.at[slot], ps.at[k], pr.at[slot], col_id(z))

    def ug_cp(k, z, slot):
        return rcopy(ug_send.at[k], ug_recv.at[slot], gs.at[k], gr.at[slot], col_id(z))

    def hist_cp(k, q, slot):
        return rcopy(hist.at[me_q], hist.at[slot], hs.at[k], hr.at[slot], plane_id(q))

    def loss_cp(k, q, slot):
        return rcopy(loss_buf.at[me_q], loss_buf.at[slot], ls.at[k], lr.at[slot], plane_id(q))

    def bg_cp(k, r, slot):
        dev = {"bank": 2 * zc + r // npair, "grp": 2 * (r % npair) + side}
        return rcopy(bg_send.at[k], bg_recv.at[slot], bs.at[k], br.at[slot], dev)

    def pre_cp(k):
        return rcopy(pre_send.at[k], pre_recv.at[k], xs.at[k], xr.at[k], sibling)

    def half_rows(i):
        return pl.ds(pl.multiple_of(i * half, half), half)

    bank_cp = rcopy(
        bank_ref.at[half_rows(side)], pbank.at[half_rows(side)],
        bank_sem.at[0], bank_sem.at[1], {"bank": 2 * zc + 1 - par, "grp": me_g},
    )
    forward_cp = rcopy(
        pbank.at[half_rows(side)], pbank.at[half_rows(side)],
        bank_sem.at[2], bank_sem.at[3], sibling,
    )
    forwarded_cp = rcopy(
        pbank.at[half_rows(1 - side)], pbank.at[half_rows(1 - side)],
        bank_sem.at[2], bank_sem.at[3], sibling,
    )

    barrier = pltpu.get_barrier_semaphore()
    for k in range(1, nz):
        pl.semaphore_signal(barrier, inc=1, device_id=col_id(col(k)), device_id_type=MESH)
    for k in range(1, nq):
        pl.semaphore_signal(barrier, inc=1, device_id=plane_id(plane(k)), device_id_type=MESH)

    loads = [
        pltpu.make_async_copy(src, dst, local.at[i])
        for i, (src, dst) in enumerate((
            (pos_hbm, pos_ref), (coh_hbm, coh_ref),
            (users_hbm, allu.at[rows(zc)]), (bank_hbm, bank_ref),
        ))
    ]
    for load in loads:
        load.start()
    for load in loads[:2]:
        load.wait()
    top_rows = lax.broadcasted_iota(jnp.int32, (8, per_dev), 0) == 0
    own_meta = jnp.where(top_rows, pos_ref[...], coh_ref[...])
    meta_own[...] = own_meta
    meta[zc] = own_meta
    item_ids = lax.broadcasted_iota(jnp.int32, (items, per_dev), 0)
    banks = (bank_ref, pbank)
    base = (me_b * items, (2 * zc + 1 - par) * items)

    def hot_of(h, z):
        return item_ids == meta[z, 0:1, :] - base[h]

    def block(h, z):
        logits = lax.dot_general(
            banks[h][...], allu[rows(z), :], (((1,), (1,)), ((), ())),
            preferred_element_type=F32,
        )
        top = jnp.max(logits, axis=0, keepdims=True)
        e = jnp.exp(logits - top)
        ex[h, z] = e
        loc_max[h, pl.ds(z, 1), :] = top
        loc_sum[h, pl.ds(z, 1), :] = jnp.sum(e, axis=0, keepdims=True)
        loc_pos[h, pl.ds(z, 1), :] = jnp.sum(
            jnp.where(hot_of(h, z), logits, F32(0.0)), axis=0, keepdims=True
        )

    for load in loads[2:]:
        load.wait()
    pl.semaphore_wait(barrier, nz - 1 + nq - 1)
    for k in range(1, nz):
        meta_cp(k, col(k), zc).start()
    bank_cp.start()
    for k in range(1, nz):
        users_cp(k, col(k), zc).start()
    block(0, zc)

    coh_ids = lax.broadcasted_iota(jnp.int32, (NCOH, per_dev), 0)
    for k in range(1, nz):
        z = col(nz - k)
        meta_cp(k, z, z).wait_recv()

    def count(z, acc):
        return acc + (coh_ids == meta[z, 1:2, :]).astype(F32)

    hist[me_q] = lax.fori_loop(0, nz, count, jnp.zeros((NCOH, per_dev), F32))
    for k in range(1, nq):
        hist_cp(k, plane(k), me_q).start()

    bank_cp.wait_recv()
    forward_cp.start()
    near = col(nz - 1)
    users_cp(1, near, near).wait_recv()
    block(0, near)
    forwarded_cp.wait_recv()
    block(1, zc)
    block(1, near)

    def arriving(k, carry):
        z = col(nz - k)
        users_cp(k, z, z).wait_recv()
        block(0, z)
        block(1, z)
        return carry

    lax.fori_loop(2, nz, arriving, 0)

    m0, m1 = loc_max[0], loc_max[1]
    m = jnp.maximum(m0, m1)
    s = loc_sum[0] * jnp.exp(m0 - m) + loc_sum[1] * jnp.exp(m1 - m)
    stat[zc, 0:nz, :] = m
    stat[zc, nz : 2 * nz, :] = s
    posl[zc] = jnp.zeros(posl.shape[1:], F32)
    posl[zc, 0:nz, :] = loc_pos[0] + loc_pos[1]
    for k in range(1, nz):
        stat_cp(k, col(k), zc).start()
    for k in range(1, nz):
        posl_cp(k, col(k), zc).start()

    def turned(left, h):
        return lax.dot_general(
            left.astype(BF16), banks[h][...], (((0,), (0,)), ((), ())),
            preferred_element_type=F32,
        )

    def ahead(z, carry):
        for h in range(2):
            et[h, z] = turned(ex[h, z], h)
        ones = [jnp.where(hot_of(h, z), F32(1.0), F32(0.0)) for h in range(2)]
        ht[z] = turned(ones[0], 0) + turned(ones[1], 1)
        return carry

    lax.fori_loop(0, nz, ahead, 0)

    for k in range(1, nq):
        q = plane(nq - k)
        hist_cp(k, q, q).wait_recv()
    total = hist[0]
    for q in range(1, nq):
        total = total + hist[q]
    counts = jnp.sum(total, axis=1, keepdims=True)
    scale = F32(per_dev * nz * nq) / NCOH

    def weigh(z, carry):
        own = jnp.sum(
            jnp.where(coh_ids == meta[z, 1:2, :], counts, F32(0.0)), axis=0, keepdims=True
        )
        wt[pl.ds(z, 1), :] = scale / own
        return carry

    lax.fori_loop(0, nz, weigh, 0)
    for k in range(1, nz):
        z = col(nz - k)
        stat_cp(k, z, z).wait_recv()
    top = stat[0, 0:nz, :]
    for z in range(1, nz):
        top = jnp.maximum(top, stat[z, 0:nz, :])
    tot = jnp.zeros_like(top)
    for z in range(nz):
        tot = tot + stat[z, nz : 2 * nz, :] * jnp.exp(stat[z, 0:nz, :] - top)
    lse = top + jnp.log(tot)
    cw[0] = wt[...] * jnp.exp(m0 - lse)
    cw[1] = wt[...] * jnp.exp(m1 - lse)

    def dlogits(h, z):
        w = wt[pl.ds(z, 1), :]
        d = ex[h, z] * cw[h, pl.ds(z, 1), :] - jnp.where(hot_of(h, z), w, F32(0.0))
        dl[h, :, rows(z)] = d.astype(BF16)

    eight = lax.broadcasted_iota(jnp.int32, (8, per_dev), 0)

    def user_term(z):
        row = pl.ds(z, 1)
        c0, c1, w = cw[0, row, :], cw[1, row, :], wt[row, :]
        turn = jnp.transpose(jnp.where(eight == 0, c0, jnp.where(eight == 1, c1, w)))
        term = et[0, z] * turn[:, 0:1] + et[1, z] * turn[:, 1:2] - ht[z] * turn[:, 2:3]
        return term.astype(BF16)

    for k in range(1, nz):
        z = col(k)
        ug_send[k] = user_term(z)
        ug_cp(k, z, zc).start()

    def both(z, carry):
        dlogits(0, z)
        dlogits(1, z)
        return carry

    lax.fori_loop(0, nz, both, 0)

    def bank_term(h, g):
        left = dl[h, pl.ds(pl.multiple_of(g * share, share), share), :]
        return jnp.dot(left, allu[...], preferred_element_type=F32)

    order = [(h, i) for h in (1, 0) for i in range(npair - 1, -1, -1)]

    def pair_at(i):
        return lax.rem(pair + i, npair)

    for j, (h, i) in enumerate(order):
        pre_send[j] = bank_term(h, 2 * pair_at(i) + 1 - side).astype(BF16)
        pre_cp(j).start()
    ug_recv[zc] = user_term(zc)
    for j, (h, i) in enumerate(order):
        term = bank_term(h, 2 * pair_at(i) + side)
        pre_cp(j).wait_recv()
        term = (term + pre_recv[j].astype(F32)).astype(BF16)
        if j < nr - 1:
            bg_send[j] = term
            goal = (par if h == 0 else 1 - par) * npair + pair_at(i)
            bg_cp(j, goal, me_r).start()
        else:
            bg_recv[me_r] = term

    for k in range(1, nz):
        z = col(nz - k)
        posl_cp(k, z, z).wait_recv()
    pos = posl[0, 0:nz, :]
    for z in range(1, nz):
        pos = pos + posl[z, 0:nz, :]
    part = jnp.sum(wt[...] * (lse - pos), axis=0, keepdims=True)
    loss_buf[me_q] = jnp.broadcast_to(part, (8, per_dev))
    for k in range(1, nq):
        loss_cp(k, plane(k), me_q).start()

    for k in range(1, nz):
        z = col(nz - k)
        ug_cp(k, z, z).wait_recv()
    for k in range(1, nr):
        r = lax.rem(me_r + k, nr)
        bg_cp(k, r, r).wait_recv()
    for k in range(1, nq):
        q = plane(nq - k)
        loss_cp(k, q, q).wait_recv()

    bank_cp.wait_send()
    forward_cp.wait_send()
    for k in range(1, nz):
        z = col(k)
        for cp in (users_cp, meta_cp, stat_cp, posl_cp, ug_cp):
            cp(k, z, zc).wait_send()
    for k in range(1, nq):
        q = plane(k)
        for cp in (hist_cp, loss_cp):
            cp(k, q, me_q).wait_send()
    for j in range(nr):
        pre_cp(j).wait_send()
        if j < nr - 1:
            bg_cp(j, lax.rem(me_r + 1, nr), me_r).wait_send()


def finish(users, loss_buf, ug_recv, bg_recv, loss_ref, ug_hbm, bg_hbm, ug, bg, sem):
    copies = []
    for i, (terms, total, out) in enumerate(((ug_recv, ug, ug_hbm), (bg_recv, bg, bg_hbm))):
        acc = terms[0].astype(F32)
        for t in range(1, terms.shape[0]):
            acc = acc + terms[t].astype(F32)
        total[...] = acc
        copies.append(pltpu.make_async_copy(total, out, sem.at[i]))
        copies[-1].start()
    acc = loss_buf[0, 0:1, :]
    for q in range(1, loss_buf.shape[0]):
        acc = acc + loss_buf[q, 0:1, :]
    loss_ref[...] = jnp.sum(acc, axis=1, keepdims=True) / F32(users)
    for copy in copies:
        copy.wait()


def solution(mesh):
    n_bank, ng = mesh.shape["bank"], mesh.shape["grp"]
    nz, nq = n_bank // 2, 2 * ng

    def per_device(users, bank, positives, cohorts):
        per_dev, width = users.shape
        items = bank.shape[0]
        share = items // ng
        padded = -(-nz // 8) * 8
        dma = pltpu.SemaphoreType.DMA
        vmem = pl.BlockSpec(memory_space=pltpu.VMEM)
        anywhere = pl.BlockSpec(memory_space=pl.ANY)
        received = pl.pallas_call(
            functools.partial(kernel, nz, ng),
            out_shape=(
                pltpu.VMEM((nq, 8, per_dev), F32),
                pltpu.VMEM((nz, per_dev, width), BF16),
                pltpu.VMEM((ng, share, width), BF16),
            ),
            in_specs=[anywhere] * 4,
            out_specs=(vmem, vmem, vmem),
            scratch_shapes=[
                pltpu.VMEM((nz * per_dev, width), BF16),
                pltpu.VMEM((items, width), BF16),
                pltpu.VMEM((items, width), BF16),
                pltpu.VMEM((1, per_dev), jnp.int32),
                pltpu.VMEM((1, per_dev), jnp.int32),
                dma((4,)),
                pltpu.VMEM((8, per_dev), jnp.int32),
                pltpu.VMEM((nz, 8, per_dev), jnp.int32),
                pltpu.VMEM((2, nz, items, per_dev), F32),
                pltpu.VMEM((2, items, nz * per_dev), BF16),
                pltpu.VMEM((2, nz, per_dev), F32),
                pltpu.VMEM((2, nz, per_dev), F32),
                pltpu.VMEM((2, nz, per_dev), F32),
                pltpu.VMEM((nz, 2 * nz, per_dev), F32),
                pltpu.VMEM((nz, padded, per_dev), F32),
                pltpu.VMEM((2, nz, per_dev), F32),
                pltpu.VMEM((nz, per_dev), F32),
                pltpu.VMEM((nq, NCOH, per_dev), F32),
                pltpu.VMEM((2, nz, per_dev, width), F32),
                pltpu.VMEM((nz, per_dev, width), F32),
                pltpu.VMEM((nz, per_dev, width), BF16),
                pltpu.VMEM((ng, share, width), BF16),
                pltpu.VMEM((ng, share, width), BF16),
                pltpu.VMEM((ng, share, width), BF16),
                dma((4,)),
                dma((nz,)), dma((nz,)), dma((nz,)), dma((nz,)), dma((nz,)),
                dma((nz,)), dma((nz,)), dma((nz,)), dma((nz,)), dma((nz,)),
                dma((nq,)), dma((nq,)), dma((nq,)), dma((nq,)),
                dma((ng,)), dma((ng,)), dma((ng,)), dma((ng,)),
            ],
            compiler_params=pltpu.CompilerParams(collective_id=0, has_side_effects=True),
        )(users, bank, positives.reshape(1, per_dev), cohorts.reshape(1, per_dev))
        loss, ug, bg = pl.pallas_call(
            functools.partial(finish, per_dev * nz * nq),
            out_shape=(
                jax.ShapeDtypeStruct((1, 1), F32),
                jax.ShapeDtypeStruct((per_dev, width), F32),
                jax.ShapeDtypeStruct((share, width), F32),
            ),
            in_specs=[vmem] * 3,
            out_specs=(vmem, anywhere, anywhere),
            scratch_shapes=[
                pltpu.VMEM((per_dev, width), F32),
                pltpu.VMEM((share, width), F32),
                dma((2,)),
            ],
        )(*(pltpu.with_memory_space_constraint(x, pltpu.VMEM) for x in received))
        return loss.reshape(()), ug, bg

    placed = (P(("bank", "grp"), None), P("bank", None), P(("bank", "grp")), P(("bank", "grp")))
    return jax.shard_map(
        per_device,
        mesh=mesh,
        in_specs=placed,
        out_specs=(P(), P(("bank", "grp"), None), P(("bank", "grp"), None)),
        check_vma=False,
    )
```

```python
import functools

import jax
import jax.numpy as jnp
from jax import lax
from jax.experimental import pallas as pl
from jax.experimental.pallas import tpu as pltpu
from jax.sharding import PartitionSpec as P

NCOH = 16
MESH = pl.DeviceIdType.MESH
F32 = jnp.float32
BF16 = jnp.bfloat16


def kernel(
    nz, ng, users_hbm, bank_hbm, pos_hbm, coh_hbm,
    loss_buf, ug_recv, bg_recv,
    allu, bank_ref, pbank, pos_ref, coh_ref, local, meta_own, meta, ex, dl,
    loc_max, loc_sum, loc_pos, stat, posl, cw, wt,
    hist, et, ht, ug_send, bg_send, pre_send, pre_recv,
    bank_sem, us, ur, ms, mr, ss, sr, ps, pr, gs, gr, hs, hr, ls, lr, bs, br, xs, xr,
):
    per_dev = users_hbm.shape[0]
    items = bank_hbm.shape[0]
    share = items // ng
    nq = 2 * ng
    me_b, me_g = lax.axis_index("bank"), lax.axis_index("grp")
    zc, par = me_b // 2, me_b % 2
    me_q = par * ng + me_g
    npair, half = ng // 2, items // 2
    pair, side = me_g // 2, me_g % 2
    nr = 2 * npair
    me_r = par * npair + pair
    sibling = {"bank": me_b, "grp": 2 * pair + 1 - side}

    def col_id(z):
        return {"bank": 2 * z + par, "grp": me_g}

    def plane_id(q):
        return {"bank": 2 * zc + q // ng, "grp": q % ng}

    def col(k):
        down, up = nz - k, k - 1
        down = down - (zc - down + nz) // nz
        up = up + (up - zc + nz) // nz
        upper = (2 * zc) // nz
        return (1 - upper) * down + upper * up

    def plane(k):
        return lax.rem(me_q + k, nq)

    def rcopy(src, dst, send, recv, dev):
        return pltpu.make_async_remote_copy(
            src_ref=src, dst_ref=dst, send_sem=send, recv_sem=recv,
            device_id=dev, device_id_type=MESH,
        )

    def rows(z):
        return pl.ds(pl.multiple_of(z * per_dev, per_dev), per_dev)

    def users_cp(k, z, slot):
        return rcopy(allu.at[rows(zc)], allu.at[rows(slot)], us.at[k], ur.at[slot], col_id(z))

    def meta_cp(k, z, slot):
        return rcopy(meta_own, meta.at[slot], ms.at[k], mr.at[slot], col_id(z))

    def stat_cp(k, z, slot):
        return rcopy(stat.at[zc], stat.at[slot], ss.at[k], sr.at[slot], col_id(z))

    def posl_cp(k, z, slot):
        return rcopy(posl.at[zc], posl.at[slot], ps.at[k], pr.at[slot], col_id(z))

    def ug_cp(k, z, slot):
        return rcopy(ug_send.at[k], ug_recv.at[slot], gs.at[k], gr.at[slot], col_id(z))

    def hist_cp(k, q, slot):
        return rcopy(hist.at[me_q], hist.at[slot], hs.at[k], hr.at[slot], plane_id(q))

    def loss_cp(k, q, slot):
        return rcopy(loss_buf.at[me_q], loss_buf.at[slot], ls.at[k], lr.at[slot], plane_id(q))

    def bg_cp(k, r, slot):
        dev = {"bank": 2 * zc + r // npair, "grp": 2 * (r % npair) + side}
        return rcopy(bg_send.at[k], bg_recv.at[slot], bs.at[k], br.at[slot], dev)

    def pre_cp(k):
        return rcopy(pre_send.at[k], pre_recv.at[k], xs.at[k], xr.at[k], sibling)

    def half_rows(i):
        return pl.ds(pl.multiple_of(i * half, half), half)

    bank_cp = rcopy(
        bank_ref.at[half_rows(side)], pbank.at[half_rows(side)],
        bank_sem.at[0], bank_sem.at[1], {"bank": 2 * zc + 1 - par, "grp": me_g},
    )
    forward_cp = rcopy(
        pbank.at[half_rows(side)], pbank.at[half_rows(side)],
        bank_sem.at[2], bank_sem.at[3], sibling,
    )
    forwarded_cp = rcopy(
        pbank.at[half_rows(1 - side)], pbank.at[half_rows(1 - side)],
        bank_sem.at[2], bank_sem.at[3], sibling,
    )

    barrier = pltpu.get_barrier_semaphore()
    for k in range(1, nz):
        pl.semaphore_signal(barrier, inc=1, device_id=col_id(col(k)), device_id_type=MESH)
    for k in range(1, nq):
        pl.semaphore_signal(barrier, inc=1, device_id=plane_id(plane(k)), device_id_type=MESH)

    loads = [
        pltpu.make_async_copy(src, dst, local.at[i])
        for i, (src, dst) in enumerate((
            (pos_hbm, pos_ref), (coh_hbm, coh_ref),
            (users_hbm, allu.at[rows(zc)]), (bank_hbm, bank_ref),
        ))
    ]
    for load in loads:
        load.start()
    for load in loads[:2]:
        load.wait()
    top_rows = lax.broadcasted_iota(jnp.int32, (8, per_dev), 0) == 0
    own_meta = jnp.where(top_rows, pos_ref[...], coh_ref[...])
    meta_own[...] = own_meta
    meta[zc] = own_meta
    item_ids = lax.broadcasted_iota(jnp.int32, (items, per_dev), 0)
    banks = (bank_ref, pbank)
    base = (me_b * items, (2 * zc + 1 - par) * items)

    def hot_of(h, z):
        return item_ids == meta[z, 0:1, :] - base[h]

    def block(h, z):
        logits = lax.dot_general(
            banks[h][...], allu[rows(z), :], (((1,), (1,)), ((), ())),
            preferred_element_type=F32,
        )
        top = jnp.max(logits, axis=0, keepdims=True)
        e = jnp.exp(logits - top)
        ex[h, z] = e
        loc_max[h, pl.ds(z, 1), :] = top
        loc_sum[h, pl.ds(z, 1), :] = jnp.sum(e, axis=0, keepdims=True)
        loc_pos[h, pl.ds(z, 1), :] = jnp.sum(
            jnp.where(hot_of(h, z), logits, F32(0.0)), axis=0, keepdims=True
        )

    for load in loads[2:]:
        load.wait()
    block(0, zc)
    pl.semaphore_wait(barrier, nz - 1 + nq - 1)
    for k in range(1, nz):
        meta_cp(k, col(k), zc).start()
    bank_cp.start()
    for k in range(1, nz):
        users_cp(k, col(k), zc).start()

    coh_ids = lax.broadcasted_iota(jnp.int32, (NCOH, per_dev), 0)
    for k in range(1, nz):
        z = col(nz - k)
        meta_cp(k, z, z).wait_recv()

    def count(z, acc):
        return acc + (coh_ids == meta[z, 1:2, :]).astype(F32)

    hist[me_q] = lax.fori_loop(0, nz, count, jnp.zeros((NCOH, per_dev), F32))
    for k in range(1, nq):
        hist_cp(k, plane(k), me_q).start()

    bank_cp.wait_recv()
    forward_cp.start()
    near = col(nz - 1)
    users_cp(1, near, near).wait_recv()
    block(0, near)
    forwarded_cp.wait_recv()
    block(1, zc)
    block(1, near)

    def arriving(k, carry):
        z = col(nz - k)
        users_cp(k, z, z).wait_recv()
        block(0, z)
        block(1, z)
        return carry

    lax.fori_loop(2, nz, arriving, 0)

    m0, m1 = loc_max[0], loc_max[1]
    m = jnp.maximum(m0, m1)
    s = loc_sum[0] * jnp.exp(m0 - m) + loc_sum[1] * jnp.exp(m1 - m)
    stat[zc, 0:nz, :] = m
    stat[zc, nz : 2 * nz, :] = s
    posl[zc] = jnp.zeros(posl.shape[1:], F32)
    posl[zc, 0:nz, :] = loc_pos[0] + loc_pos[1]
    for k in range(1, nz):
        stat_cp(k, col(k), zc).start()
    for k in range(1, nz):
        posl_cp(k, col(k), zc).start()

    def turned(left, h):
        return lax.dot_general(
            left.astype(BF16), banks[h][...], (((0,), (0,)), ((), ())),
            preferred_element_type=F32,
        )

    def ahead(z, carry):
        for h in range(2):
            et[h, z] = turned(ex[h, z], h)
        ones = [jnp.where(hot_of(h, z), F32(1.0), F32(0.0)) for h in range(2)]
        ht[z] = turned(ones[0], 0) + turned(ones[1], 1)
        return carry

    lax.fori_loop(0, nz, ahead, 0)

    for k in range(1, nq):
        q = plane(nq - k)
        hist_cp(k, q, q).wait_recv()
    total = hist[0]
    for q in range(1, nq):
        total = total + hist[q]
    counts = jnp.sum(total, axis=1, keepdims=True)
    scale = F32(per_dev * nz * nq) / NCOH

    def weigh(z, carry):
        own = jnp.sum(
            jnp.where(coh_ids == meta[z, 1:2, :], counts, F32(0.0)), axis=0, keepdims=True
        )
        wt[pl.ds(z, 1), :] = scale / own
        return carry

    lax.fori_loop(0, nz, weigh, 0)
    for k in range(1, nz):
        z = col(nz - k)
        stat_cp(k, z, z).wait_recv()
    top = stat[0, 0:nz, :]
    for z in range(1, nz):
        top = jnp.maximum(top, stat[z, 0:nz, :])
    tot = jnp.zeros_like(top)
    for z in range(nz):
        tot = tot + stat[z, nz : 2 * nz, :] * jnp.exp(stat[z, 0:nz, :] - top)
    lse = top + jnp.log(tot)
    cw[0] = wt[...] * jnp.exp(m0 - lse)
    cw[1] = wt[...] * jnp.exp(m1 - lse)

    def dlogits(h, z):
        w = wt[pl.ds(z, 1), :]
        d = ex[h, z] * cw[h, pl.ds(z, 1), :] - jnp.where(hot_of(h, z), w, F32(0.0))
        dl[h, :, rows(z)] = d.astype(BF16)

    eight = lax.broadcasted_iota(jnp.int32, (8, per_dev), 0)

    def user_term(z):
        row = pl.ds(z, 1)
        c0, c1, w = cw[0, row, :], cw[1, row, :], wt[row, :]
        turn = jnp.transpose(jnp.where(eight == 0, c0, jnp.where(eight == 1, c1, w)))
        term = et[0, z] * turn[:, 0:1] + et[1, z] * turn[:, 1:2] - ht[z] * turn[:, 2:3]
        return term.astype(BF16)

    def form(h):
        def step(z, carry):
            dlogits(h, z)
            return carry

        lax.fori_loop(0, nz, step, 0, unroll=nz <= 4)

    def bank_term(h, g):
        left = dl[h, pl.ds(pl.multiple_of(g * share, share), share), :]
        return jnp.dot(left, allu[...], preferred_element_type=F32)

    order = [(h, i) for h in (1, 0) for i in range(npair - 1, -1, -1)]

    def pair_at(i):
        return lax.rem(pair + i, npair)

    def give(j):
        h, i = order[j]
        pre_send[j] = bank_term(h, 2 * pair_at(i) + 1 - side).astype(BF16)
        pre_cp(j).start()

    form(1)
    for j in range(npair):
        give(j)
    for k in range(1, nz):
        z = col(k)
        ug_send[k] = user_term(z)
        ug_cp(k, z, zc).start()

    for k in range(1, nz):
        z = col(nz - k)
        posl_cp(k, z, z).wait_recv()
    pos = posl[0, 0:nz, :]
    for z in range(1, nz):
        pos = pos + posl[z, 0:nz, :]
    part = jnp.sum(wt[...] * (lse - pos), axis=0, keepdims=True)
    loss_buf[me_q] = jnp.broadcast_to(part, (8, per_dev))
    for k in range(1, nq):
        loss_cp(k, plane(k), me_q).start()
    form(0)
    for j, (h, i) in enumerate(order):
        if j < npair:
            give(npair + j)
        term = bank_term(h, 2 * pair_at(i) + side)
        pre_cp(j).wait_recv()
        term = (term + pre_recv[j].astype(F32)).astype(BF16)
        if j < nr - 1:
            bg_send[j] = term
            goal = (par if h == 0 else 1 - par) * npair + pair_at(i)
            bg_cp(j, goal, me_r).start()
        else:
            bg_recv[me_r] = term
    ug_recv[zc] = user_term(zc)

    for k in range(1, nz):
        z = col(nz - k)
        ug_cp(k, z, z).wait_recv()
    for k in range(1, nr):
        r = lax.rem(me_r + k, nr)
        bg_cp(k, r, r).wait_recv()
    for k in range(1, nq):
        q = plane(nq - k)
        loss_cp(k, q, q).wait_recv()

    bank_cp.wait_send()
    forward_cp.wait_send()
    for k in range(1, nz):
        z = col(k)
        for cp in (users_cp, meta_cp, stat_cp, posl_cp, ug_cp):
            cp(k, z, zc).wait_send()
    for k in range(1, nq):
        q = plane(k)
        for cp in (hist_cp, loss_cp):
            cp(k, q, me_q).wait_send()
    for j in range(nr):
        pre_cp(j).wait_send()
        if j < nr - 1:
            bg_cp(j, lax.rem(me_r + 1, nr), me_r).wait_send()


def finish(users, loss_buf, ug_recv, bg_recv, loss_ref, ug_hbm, bg_hbm, ug, bg, sem):
    copies = []
    for i, (terms, total, out) in enumerate(((ug_recv, ug, ug_hbm), (bg_recv, bg, bg_hbm))):
        acc = terms[0].astype(F32)
        for t in range(1, terms.shape[0]):
            acc = acc + terms[t].astype(F32)
        total[...] = acc
        copies.append(pltpu.make_async_copy(total, out, sem.at[i]))
        copies[-1].start()
    acc = loss_buf[0, 0:1, :]
    for q in range(1, loss_buf.shape[0]):
        acc = acc + loss_buf[q, 0:1, :]
    loss_ref[...] = jnp.sum(acc, axis=1, keepdims=True) / F32(users)
    for copy in copies:
        copy.wait()


def solution(mesh):
    n_bank, ng = mesh.shape["bank"], mesh.shape["grp"]
    nz, nq = n_bank // 2, 2 * ng

    def per_device(users, bank, positives, cohorts):
        per_dev, width = users.shape
        items = bank.shape[0]
        share = items // ng
        padded = -(-nz // 8) * 8
        dma = pltpu.SemaphoreType.DMA
        vmem = pl.BlockSpec(memory_space=pltpu.VMEM)
        anywhere = pl.BlockSpec(memory_space=pl.ANY)
        received = pl.pallas_call(
            functools.partial(kernel, nz, ng),
            out_shape=(
                pltpu.VMEM((nq, 8, per_dev), F32),
                pltpu.VMEM((nz, per_dev, width), BF16),
                pltpu.VMEM((ng, share, width), BF16),
            ),
            in_specs=[anywhere] * 4,
            out_specs=(vmem, vmem, vmem),
            scratch_shapes=[
                pltpu.VMEM((nz * per_dev, width), BF16),
                pltpu.VMEM((items, width), BF16),
                pltpu.VMEM((items, width), BF16),
                pltpu.VMEM((1, per_dev), jnp.int32),
                pltpu.VMEM((1, per_dev), jnp.int32),
                dma((4,)),
                pltpu.VMEM((8, per_dev), jnp.int32),
                pltpu.VMEM((nz, 8, per_dev), jnp.int32),
                pltpu.VMEM((2, nz, items, per_dev), F32),
                pltpu.VMEM((2, items, nz * per_dev), BF16),
                pltpu.VMEM((2, nz, per_dev), F32),
                pltpu.VMEM((2, nz, per_dev), F32),
                pltpu.VMEM((2, nz, per_dev), F32),
                pltpu.VMEM((nz, 2 * nz, per_dev), F32),
                pltpu.VMEM((nz, padded, per_dev), F32),
                pltpu.VMEM((2, nz, per_dev), F32),
                pltpu.VMEM((nz, per_dev), F32),
                pltpu.VMEM((nq, NCOH, per_dev), F32),
                pltpu.VMEM((2, nz, per_dev, width), F32),
                pltpu.VMEM((nz, per_dev, width), F32),
                pltpu.VMEM((nz, per_dev, width), BF16),
                pltpu.VMEM((ng, share, width), BF16),
                pltpu.VMEM((ng, share, width), BF16),
                pltpu.VMEM((ng, share, width), BF16),
                dma((4,)),
                dma((nz,)), dma((nz,)), dma((nz,)), dma((nz,)), dma((nz,)),
                dma((nz,)), dma((nz,)), dma((nz,)), dma((nz,)), dma((nz,)),
                dma((nq,)), dma((nq,)), dma((nq,)), dma((nq,)),
                dma((ng,)), dma((ng,)), dma((ng,)), dma((ng,)),
            ],
            compiler_params=pltpu.CompilerParams(collective_id=0, has_side_effects=True),
        )(users, bank, positives.reshape(1, per_dev), cohorts.reshape(1, per_dev))
        loss, ug, bg = pl.pallas_call(
            functools.partial(finish, per_dev * nz * nq),
            out_shape=(
                jax.ShapeDtypeStruct((1, 1), F32),
                jax.ShapeDtypeStruct((per_dev, width), F32),
                jax.ShapeDtypeStruct((share, width), F32),
            ),
            in_specs=[vmem] * 3,
            out_specs=(vmem, anywhere, anywhere),
            scratch_shapes=[
                pltpu.VMEM((per_dev, width), F32),
                pltpu.VMEM((share, width), F32),
                dma((2,)),
            ],
        )(*(pltpu.with_memory_space_constraint(x, pltpu.VMEM) for x in received))
        return loss.reshape(()), ug, bg

    placed = (P(("bank", "grp"), None), P("bank", None), P(("bank", "grp")), P(("bank", "grp")))
    return jax.shard_map(
        per_device,
        mesh=mesh,
        in_specs=placed,
        out_specs=(P(), P(("bank", "grp"), None), P(("bank", "grp"), None)),
        check_vma=False,
    )
```

```python
import functools

import jax
import jax.numpy as jnp
from jax import lax
from jax.experimental import pallas as pl
from jax.experimental.pallas import tpu as pltpu
from jax.sharding import PartitionSpec as P

NCOH = 16
MESH = pl.DeviceIdType.MESH
F32 = jnp.float32
BF16 = jnp.bfloat16


def kernel(
    nz, ng, users_hbm, bank_hbm, pos_hbm, coh_hbm,
    loss_buf, ug_sum, bg_recv,
    allu, bank_ref, pbank, pos_ref, coh_ref, local, meta_own, meta, ex, dl,
    loc_max, loc_sum, loc_pos, stat, posl, cw, wt,
    hist, et, ht, ug_recv, ug_send, bg_send, pre_send, pre_recv,
    bank_sem, us, ur, ms, mr, ss, sr, ps, pr, gs, gr, hs, hr, ls, lr, bs, br, xs, xr,
):
    per_dev = users_hbm.shape[0]
    items = bank_hbm.shape[0]
    share = items // ng
    nq = 2 * ng
    me_b, me_g = lax.axis_index("bank"), lax.axis_index("grp")
    zc, par = me_b // 2, me_b % 2
    me_q = par * ng + me_g
    npair, half = ng // 2, items // 2
    pair, side = me_g // 2, me_g % 2
    nr = 2 * npair
    me_r = par * npair + pair
    sibling = {"bank": me_b, "grp": 2 * pair + 1 - side}

    def col_id(z):
        return {"bank": 2 * z + par, "grp": me_g}

    def plane_id(q):
        return {"bank": 2 * zc + q // ng, "grp": q % ng}

    def col(k):
        down, up = nz - k, k - 1
        down = down - (zc - down + nz) // nz
        up = up + (up - zc + nz) // nz
        upper = (2 * zc) // nz
        return (1 - upper) * down + upper * up

    def plane(k):
        return lax.rem(me_q + k, nq)

    def rcopy(src, dst, send, recv, dev):
        return pltpu.make_async_remote_copy(
            src_ref=src, dst_ref=dst, send_sem=send, recv_sem=recv,
            device_id=dev, device_id_type=MESH,
        )

    def rows(z):
        return pl.ds(pl.multiple_of(z * per_dev, per_dev), per_dev)

    def users_cp(k, z, slot):
        return rcopy(allu.at[rows(zc)], allu.at[rows(slot)], us.at[k], ur.at[slot], col_id(z))

    def meta_cp(k, z, slot):
        return rcopy(meta_own, meta.at[slot], ms.at[k], mr.at[slot], col_id(z))

    def stat_cp(k, z, slot):
        return rcopy(stat.at[zc], stat.at[slot], ss.at[k], sr.at[slot], col_id(z))

    def posl_cp(k, z, slot):
        return rcopy(posl.at[zc], posl.at[slot], ps.at[k], pr.at[slot], col_id(z))

    def ug_cp(k, z, slot):
        return rcopy(ug_send.at[k], ug_recv.at[slot], gs.at[k], gr.at[slot], col_id(z))

    def hist_cp(k, q, slot):
        return rcopy(hist.at[me_q], hist.at[slot], hs.at[k], hr.at[slot], plane_id(q))

    def loss_cp(k, q, slot):
        return rcopy(loss_buf.at[me_q], loss_buf.at[slot], ls.at[k], lr.at[slot], plane_id(q))

    def bg_cp(k, r, slot):
        dev = {"bank": 2 * zc + r // npair, "grp": 2 * (r % npair) + side}
        return rcopy(bg_send.at[k], bg_recv.at[slot], bs.at[k], br.at[slot], dev)

    def pre_cp(k):
        return rcopy(pre_send.at[k], pre_recv.at[k], xs.at[k], xr.at[k], sibling)

    def half_rows(i):
        return pl.ds(pl.multiple_of(i * half, half), half)

    bank_cp = rcopy(
        bank_ref.at[half_rows(side)], pbank.at[half_rows(side)],
        bank_sem.at[0], bank_sem.at[1], {"bank": 2 * zc + 1 - par, "grp": me_g},
    )
    forward_cp = rcopy(
        pbank.at[half_rows(side)], pbank.at[half_rows(side)],
        bank_sem.at[2], bank_sem.at[3], sibling,
    )
    forwarded_cp = rcopy(
        pbank.at[half_rows(1 - side)], pbank.at[half_rows(1 - side)],
        bank_sem.at[2], bank_sem.at[3], sibling,
    )

    barrier = pltpu.get_barrier_semaphore()
    for k in range(1, nz):
        pl.semaphore_signal(barrier, inc=1, device_id=col_id(col(k)), device_id_type=MESH)
    for k in range(1, nq):
        pl.semaphore_signal(barrier, inc=1, device_id=plane_id(plane(k)), device_id_type=MESH)

    loads = [
        pltpu.make_async_copy(src, dst, local.at[i])
        for i, (src, dst) in enumerate((
            (pos_hbm, pos_ref), (coh_hbm, coh_ref),
            (users_hbm, allu.at[rows(zc)]), (bank_hbm, bank_ref),
        ))
    ]
    for load in loads:
        load.start()
    for load in loads[:2]:
        load.wait()
    top_rows = lax.broadcasted_iota(jnp.int32, (8, per_dev), 0) == 0
    own_meta = jnp.where(top_rows, pos_ref[...], coh_ref[...])
    meta_own[...] = own_meta
    meta[zc] = own_meta
    item_ids = lax.broadcasted_iota(jnp.int32, (items, per_dev), 0)
    banks = (bank_ref, pbank)
    base = (me_b * items, (2 * zc + 1 - par) * items)

    def hot_of(h, z):
        return item_ids == meta[z, 0:1, :] - base[h]

    def block(h, z):
        logits = lax.dot_general(
            banks[h][...], allu[rows(z), :], (((1,), (1,)), ((), ())),
            preferred_element_type=F32,
        )
        top = jnp.max(logits, axis=0, keepdims=True)
        e = jnp.exp(logits - top)
        ex[h, z] = e
        loc_max[h, pl.ds(z, 1), :] = top
        loc_sum[h, pl.ds(z, 1), :] = jnp.sum(e, axis=0, keepdims=True)
        loc_pos[h, pl.ds(z, 1), :] = jnp.sum(
            jnp.where(hot_of(h, z), logits, F32(0.0)), axis=0, keepdims=True
        )

    for load in loads[2:]:
        load.wait()
    block(0, zc)
    pl.semaphore_wait(barrier, nz - 1 + nq - 1)
    for k in range(1, nz):
        meta_cp(k, col(k), zc).start()
    bank_cp.start()
    for k in range(1, nz):
        users_cp(k, col(k), zc).start()

    coh_ids = lax.broadcasted_iota(jnp.int32, (NCOH, per_dev), 0)
    for k in range(1, nz):
        z = col(nz - k)
        meta_cp(k, z, z).wait_recv()

    def count(z, acc):
        return acc + (coh_ids == meta[z, 1:2, :]).astype(F32)

    hist[me_q] = lax.fori_loop(0, nz, count, jnp.zeros((NCOH, per_dev), F32))
    for k in range(1, nq):
        hist_cp(k, plane(k), me_q).start()

    bank_cp.wait_recv()
    forward_cp.start()
    near = col(nz - 1)
    users_cp(1, near, near).wait_recv()
    block(0, near)
    forwarded_cp.wait_recv()
    block(1, zc)
    block(1, near)

    def arriving(k, carry):
        z = col(nz - k)
        users_cp(k, z, z).wait_recv()
        block(0, z)
        block(1, z)
        return carry

    lax.fori_loop(2, nz, arriving, 0)

    m0, m1 = loc_max[0], loc_max[1]
    m = jnp.maximum(m0, m1)
    s = loc_sum[0] * jnp.exp(m0 - m) + loc_sum[1] * jnp.exp(m1 - m)
    stat[zc, 0:nz, :] = m
    stat[zc, nz : 2 * nz, :] = s
    posl[zc] = jnp.zeros(posl.shape[1:], F32)
    posl[zc, 0:nz, :] = loc_pos[0] + loc_pos[1]
    for k in range(1, nz):
        stat_cp(k, col(k), zc).start()
    for k in range(1, nz):
        posl_cp(k, col(k), zc).start()

    def turned(left, h):
        return lax.dot_general(
            left.astype(BF16), banks[h][...], (((0,), (0,)), ((), ())),
            preferred_element_type=F32,
        )

    def ahead(z, carry):
        for h in range(2):
            et[h, z] = turned(ex[h, z], h)
        ones = [jnp.where(hot_of(h, z), F32(1.0), F32(0.0)) for h in range(2)]
        ht[z] = turned(ones[0], 0) + turned(ones[1], 1)
        return carry

    lax.fori_loop(0, nz, ahead, 0)

    for k in range(1, nq):
        q = plane(nq - k)
        hist_cp(k, q, q).wait_recv()
    total = hist[0]
    for q in range(1, nq):
        total = total + hist[q]
    counts = jnp.sum(total, axis=1, keepdims=True)
    scale = F32(per_dev * nz * nq) / NCOH

    def weigh(z, carry):
        own = jnp.sum(
            jnp.where(coh_ids == meta[z, 1:2, :], counts, F32(0.0)), axis=0, keepdims=True
        )
        wt[pl.ds(z, 1), :] = scale / own
        return carry

    lax.fori_loop(0, nz, weigh, 0)
    for k in range(1, nz):
        z = col(nz - k)
        stat_cp(k, z, z).wait_recv()
    top = stat[0, 0:nz, :]
    for z in range(1, nz):
        top = jnp.maximum(top, stat[z, 0:nz, :])
    tot = jnp.zeros_like(top)
    for z in range(nz):
        tot = tot + stat[z, nz : 2 * nz, :] * jnp.exp(stat[z, 0:nz, :] - top)
    lse = top + jnp.log(tot)
    cw[0] = wt[...] * jnp.exp(m0 - lse)
    cw[1] = wt[...] * jnp.exp(m1 - lse)

    def dlogits(h, z):
        w = wt[pl.ds(z, 1), :]
        d = ex[h, z] * cw[h, pl.ds(z, 1), :] - jnp.where(hot_of(h, z), w, F32(0.0))
        dl[h, :, rows(z)] = d.astype(BF16)

    eight = lax.broadcasted_iota(jnp.int32, (8, per_dev), 0)

    def user_term(z):
        row = pl.ds(z, 1)
        c0, c1, w = cw[0, row, :], cw[1, row, :], wt[row, :]
        turn = jnp.transpose(jnp.where(eight == 0, c0, jnp.where(eight == 1, c1, w)))
        term = et[0, z] * turn[:, 0:1] + et[1, z] * turn[:, 1:2] - ht[z] * turn[:, 2:3]
        return term.astype(BF16)

    def form(h):
        def step(z, carry):
            dlogits(h, z)
            return carry

        lax.fori_loop(0, nz, step, 0, unroll=nz <= 4)

    def bank_term(h, g):
        left = dl[h, pl.ds(pl.multiple_of(g * share, share), share), :]
        return jnp.dot(left, allu[...], preferred_element_type=F32)

    order = [(h, i) for h in (1, 0) for i in range(npair - 1, -1, -1)]

    def pair_at(i):
        return lax.rem(pair + i, npair)

    def give(j):
        h, i = order[j]
        pre_send[j] = bank_term(h, 2 * pair_at(i) + 1 - side).astype(BF16)
        pre_cp(j).start()

    form(1)
    for j in range(npair):
        give(j)
    for k in range(1, nz):
        z = col(k)
        ug_send[k] = user_term(z)
        ug_cp(k, z, zc).start()

    for k in range(1, nz):
        z = col(nz - k)
        posl_cp(k, z, z).wait_recv()
    pos = posl[0, 0:nz, :]
    for z in range(1, nz):
        pos = pos + posl[z, 0:nz, :]
    part = jnp.sum(wt[...] * (lse - pos), axis=0, keepdims=True)
    loss_buf[me_q] = jnp.broadcast_to(part, (8, per_dev))
    for k in range(1, nq):
        loss_cp(k, plane(k), me_q).start()
    form(0)
    for j, (h, i) in enumerate(order):
        if j < npair:
            give(npair + j)
        term = bank_term(h, 2 * pair_at(i) + side)
        pre_cp(j).wait_recv()
        term = (term + pre_recv[j].astype(F32)).astype(BF16)
        if j < nr - 1:
            bg_send[j] = term
            goal = (par if h == 0 else 1 - par) * npair + pair_at(i)
            bg_cp(j, goal, me_r).start()
        else:
            bg_recv[me_r] = term
    ug_recv[zc] = user_term(zc)

    for k in range(1, nz):
        z = col(nz - k)
        ug_cp(k, z, z).wait_recv()
    acc = ug_recv[0].astype(F32)
    for z in range(1, nz):
        acc = acc + ug_recv[z].astype(F32)
    ug_sum[...] = acc
    for k in range(1, nr):
        r = lax.rem(me_r + k, nr)
        bg_cp(k, r, r).wait_recv()
    for k in range(1, nq):
        q = plane(nq - k)
        loss_cp(k, q, q).wait_recv()

    bank_cp.wait_send()
    forward_cp.wait_send()
    for k in range(1, nz):
        z = col(k)
        for cp in (users_cp, meta_cp, stat_cp, posl_cp, ug_cp):
            cp(k, z, zc).wait_send()
    for k in range(1, nq):
        q = plane(k)
        for cp in (hist_cp, loss_cp):
            cp(k, q, me_q).wait_send()
    for j in range(nr):
        pre_cp(j).wait_send()
        if j < nr - 1:
            bg_cp(j, lax.rem(me_r + 1, nr), me_r).wait_send()


def finish(users, loss_buf, ug, bg_recv, loss_ref, ug_hbm, bg_hbm, bg, sem):
    copies = [
        pltpu.make_async_copy(ug, ug_hbm, sem.at[0]),
        pltpu.make_async_copy(bg, bg_hbm, sem.at[1]),
    ]
    copies[0].start()
    acc = bg_recv[0].astype(F32)
    for t in range(1, bg_recv.shape[0]):
        acc = acc + bg_recv[t].astype(F32)
    bg[...] = acc
    copies[1].start()
    acc = loss_buf[0, 0:1, :]
    for q in range(1, loss_buf.shape[0]):
        acc = acc + loss_buf[q, 0:1, :]
    loss_ref[...] = jnp.sum(acc, axis=1, keepdims=True) / F32(users)
    for copy in copies:
        copy.wait()


def solution(mesh):
    n_bank, ng = mesh.shape["bank"], mesh.shape["grp"]
    nz, nq = n_bank // 2, 2 * ng

    def per_device(users, bank, positives, cohorts):
        per_dev, width = users.shape
        items = bank.shape[0]
        share = items // ng
        padded = -(-nz // 8) * 8
        dma = pltpu.SemaphoreType.DMA
        vmem = pl.BlockSpec(memory_space=pltpu.VMEM)
        anywhere = pl.BlockSpec(memory_space=pl.ANY)
        received = pl.pallas_call(
            functools.partial(kernel, nz, ng),
            out_shape=(
                pltpu.VMEM((nq, 8, per_dev), F32),
                pltpu.VMEM((per_dev, width), F32),
                pltpu.VMEM((ng, share, width), BF16),
            ),
            in_specs=[anywhere] * 4,
            out_specs=(vmem, vmem, vmem),
            scratch_shapes=[
                pltpu.VMEM((nz * per_dev, width), BF16),
                pltpu.VMEM((items, width), BF16),
                pltpu.VMEM((items, width), BF16),
                pltpu.VMEM((1, per_dev), jnp.int32),
                pltpu.VMEM((1, per_dev), jnp.int32),
                dma((4,)),
                pltpu.VMEM((8, per_dev), jnp.int32),
                pltpu.VMEM((nz, 8, per_dev), jnp.int32),
                pltpu.VMEM((2, nz, items, per_dev), F32),
                pltpu.VMEM((2, items, nz * per_dev), BF16),
                pltpu.VMEM((2, nz, per_dev), F32),
                pltpu.VMEM((2, nz, per_dev), F32),
                pltpu.VMEM((2, nz, per_dev), F32),
                pltpu.VMEM((nz, 2 * nz, per_dev), F32),
                pltpu.VMEM((nz, padded, per_dev), F32),
                pltpu.VMEM((2, nz, per_dev), F32),
                pltpu.VMEM((nz, per_dev), F32),
                pltpu.VMEM((nq, NCOH, per_dev), F32),
                pltpu.VMEM((2, nz, per_dev, width), F32),
                pltpu.VMEM((nz, per_dev, width), F32),
                pltpu.VMEM((nz, per_dev, width), BF16),
                pltpu.VMEM((nz, per_dev, width), BF16),
                pltpu.VMEM((ng, share, width), BF16),
                pltpu.VMEM((ng, share, width), BF16),
                pltpu.VMEM((ng, share, width), BF16),
                dma((4,)),
                dma((nz,)), dma((nz,)), dma((nz,)), dma((nz,)), dma((nz,)),
                dma((nz,)), dma((nz,)), dma((nz,)), dma((nz,)), dma((nz,)),
                dma((nq,)), dma((nq,)), dma((nq,)), dma((nq,)),
                dma((ng,)), dma((ng,)), dma((ng,)), dma((ng,)),
            ],
            compiler_params=pltpu.CompilerParams(collective_id=0, has_side_effects=True),
        )(users, bank, positives.reshape(1, per_dev), cohorts.reshape(1, per_dev))
        loss, ug, bg = pl.pallas_call(
            functools.partial(finish, per_dev * nz * nq),
            out_shape=(
                jax.ShapeDtypeStruct((1, 1), F32),
                jax.ShapeDtypeStruct((per_dev, width), F32),
                jax.ShapeDtypeStruct((share, width), F32),
            ),
            in_specs=[vmem] * 3,
            out_specs=(vmem, anywhere, anywhere),
            scratch_shapes=[
                pltpu.VMEM((share, width), F32),
                dma((2,)),
            ],
        )(*(pltpu.with_memory_space_constraint(x, pltpu.VMEM) for x in received))
        return loss.reshape(()), ug, bg

    placed = (P(("bank", "grp"), None), P("bank", None), P(("bank", "grp")), P(("bank", "grp")))
    return jax.shard_map(
        per_device,
        mesh=mesh,
        in_specs=placed,
        out_specs=(P(), P(("bank", "grp"), None), P(("bank", "grp"), None)),
        check_vma=False,
    )
```
